128 devices in a mesh: row: 16 (over x, z_hi, core), col: 8 (over z_lo, y).
Axes of the slice: x: 4, y: 4, z: 4 (z_hi: 2, z_lo: 2; z = z_hi * 2 + z_lo), core: 2. Of those that a mesh axis runs over, the one named last changes fastest.
Arguments:
- left: bfloat16 [128, 32768], P('col', 'row'), may hold values from -15 to 15
- right: bfloat16 [128, 32768], P('row', 'col'), may hold values from -15 to 15
- weight: bfloat16 [1024, 128], replicated, may hold values from -0.1875 to 0.1875
- bias: float32 [128], replicated, may hold values from -3 to 3
- cotangent: bfloat16 [1024, 1024, 128], P('row', 'col'), may hold values from -0.1796875 to 0.1796875
Outputs:
- pair_update: bfloat16 [1024, 1024, 128], P('row', 'col')
- grad_left: bfloat16 [128, 32768], P('col', 'row')
- grad_right: bfloat16 [128, 32768], P('row', 'col')
- grad_weight: float32 [1024, 128], replicated
- grad_bias: float32 [128], replicated
The draws below stay inside these ranges and needn't reach their ends.
All inputs are finite; a program needn't handle non-finite values.
Results may differ from the reference program's by a relative error of at most 0.005.
Values may be sent and summed in bfloat16 or wider, within the bound.
No kernel may reach another device: no remote copies, remote signals or barrier semaphores. Data moves between devices by JAX's collectives and lax.ppermute only.
A program may use at most 128 MiB of HBM per device.

```python
import jax
import jax.numpy as jnp
from jax import lax

CL = 32
CP = 128
RES = 1024
SEQS = 128


def shard_levels(key, extent, shards, low, high):
    gain, own = 1.0, jax.random.fold_in(key, 6)
    for position, blocks in shards:
        steps = jnp.exp(jax.random.uniform(jax.random.fold_in(own, position), (blocks,), jnp.float32, low / len(shards), high / len(shards)))
        gain = gain * jnp.repeat(steps, extent[position] // blocks).reshape([-1 if axis == position else 1 for axis in range(len(extent))])
    return gain


def scatter_about(key, shape, spread, reach, pieces=(), held_as=jnp.bfloat16):
    entries = jax.random.normal(key, shape, jnp.float32) * spread
    if len(pieces) > 0:
        entries = shard_levels(key, shape, pieces, -0.22, 0.18) * entries
    return jnp.clip(entries, min=-reach, max=reach).astype(held_as)


def setup_inputs(seed: int = 0) -> dict:
    seeds = jax.random.split(jax.random.key(seed), 6)
    left = scatter_about(seeds[0], (SEQS, RES * CL), 3.0, 15.0, ((0, 8), (1, 16)))
    right = scatter_about(seeds[1], (SEQS, RES * CL), 3.0, 15.0, ((0, 16), (1, 8)))
    weight = scatter_about(seeds[2], (CL * CL, CP), (CL * CL) ** -0.5, 0.1875)
    bias = scatter_about(seeds[3], (CP,), 0.5, 3.0, (), jnp.float32)
    cotangent = scatter_about(seeds[4], (RES, RES, CP), 0.03, 0.1796875, ((0, 16), (1, 8)))
    return dict(left=left, right=right, weight=weight, bias=bias, cotangent=cotangent)


def reference(left, right, weight, bias, cotangent):
    lefts = left.reshape(SEQS, RES, CL)
    rights = right.reshape(SEQS, RES, CL).astype(jnp.float32)
    rblock = min(64, RES)
    nblock = RES // rblock
    scale = 1.0 / SEQS

    def step(carry, index):
        grad_w, grad_b, grad_r = carry
        lblock = lax.dynamic_slice_in_dim(lefts, (index * rblock).astype(jnp.int32), rblock, 1).astype(jnp.float32)
        outer = (jnp.einsum("sic,sje->ijce", lblock, rights) * scale).astype(jnp.bfloat16)
        outer = outer.reshape(rblock * RES, CL * CL)
        dpair = lax.dynamic_slice_in_dim(cotangent, (index * rblock).astype(jnp.int32), rblock, 0).reshape(rblock * RES, CP)
        pair = (jnp.dot(outer, weight, preferred_element_type=jnp.float32) + bias).astype(jnp.bfloat16)
        grad_outer = jnp.dot(dpair, weight.T, preferred_element_type=jnp.float32).astype(jnp.bfloat16)
        grad_w = grad_w + jnp.dot(outer.T, dpair, preferred_element_type=jnp.float32)
        grad_b = grad_b + jnp.sum(dpair.astype(jnp.float32), axis=0)
        fourway = grad_outer.reshape(rblock, RES, CL, CL).astype(jnp.float32)
        grad_l = jnp.einsum("ijce,sje->sic", fourway, rights) * scale
        grad_r = grad_r + jnp.einsum("ijce,sic->sje", fourway, lblock) * scale
        return (grad_w, grad_b, grad_r), (pair.reshape(rblock, RES, CP), grad_l)

    start = (jnp.zeros((CL * CL, CP), jnp.float32), jnp.zeros((CP,), jnp.float32), jnp.zeros((SEQS, RES, CL), jnp.float32))
    (grad_w, grad_b, grad_r), (pairs, grad_ls) = lax.scan(step, start, jnp.arange(nblock, dtype=jnp.int32))
    pair_update = pairs.reshape(RES, RES, CP)
    grad_left = grad_ls.transpose(1, 0, 2, 3).reshape(SEQS, RES * CL).astype(jnp.bfloat16)
    grad_right = grad_r.reshape(SEQS, RES * CL).astype(jnp.bfloat16)
    return pair_update, grad_left, grad_right, grad_w, grad_b
```

```python
import jax
import jax.numpy as jnp
from jax import lax
from jax.experimental import pallas as pl
from jax.experimental.pallas import tpu as pltpu
from jax.sharding import PartitionSpec as P

CL = 32
CP = 128
IB = 8
EB = 8
BF = jnp.bfloat16
F32 = jnp.float32


def dot(a, b, ca, cb):
    return lax.dot_general(a, b, (((ca,), (cb,)), ((), ())), preferred_element_type=F32)


def tile_body(l_ref, r_ref, d_ref, w_ref, wt_ref, b_ref, p_ref, gw_ref, gb_ref, gr_ref, gl_ref, o_s, g_s, acc):
    k = pl.program_id(0)
    nj = d_ref.shape[0] // IB
    scale = 1.0 / l_ref.shape[0]
    for eb in range(CL // EB):
        t = dot(l_ref[...], r_ref[:, eb * EB * nj : (eb + 1) * EB * nj], 0, 0)
        t = (t * scale).astype(BF)
        for e1 in range(EB):
            e = eb * EB + e1
            for i in range(IB):
                o_s[e * CL : (e + 1) * CL, i * nj : (i + 1) * nj] = t[
                    i * CL : (i + 1) * CL, e1 * nj : (e1 + 1) * nj
                ]
    for q in range(IB // 2):
        t = dot(w_ref[...], d_ref[q * 2 * nj : (q + 1) * 2 * nj, :], 1, 1).astype(BF)
        for i2 in range(2):
            i = q * 2 + i2
            for e in range(CL):
                g_s[i * CL : (i + 1) * CL, e * nj : (e + 1) * nj] = t[
                    e * CL : (e + 1) * CL, i2 * nj : (i2 + 1) * nj
                ]
    p_ref[...] = (dot(wt_ref[...], o_s[...], 1, 0).T + b_ref[...]).astype(BF)
    gw = dot(o_s[...], d_ref[...], 1, 0)
    gb = jnp.sum(d_ref[...].astype(F32).reshape(-1, 8, CP), axis=0)
    gl_ref[...] = (dot(g_s[...], r_ref[...], 1, 1) * scale).T.astype(BF)
    gr = dot(l_ref[...], g_s[...], 1, 0)

    @pl.when(k == 0)
    def _():
        gw_ref[...] = gw
        gb_ref[...] = gb
        acc[...] = gr

    @pl.when(k != 0)
    def _():
        gw_ref[...] += gw
        gb_ref[...] += gb
        acc[...] += gr

    @pl.when(k == pl.num_programs(0) - 1)
    def _():
        gr_ref[...] = (acc[...] * scale).astype(BF)


def tile(left, right, dpair, w, wt, bias):
    seqs, nj = right.shape[0], right.shape[1] // CL
    n = left.shape[1] // (IB * CL)
    whole = lambda *shape: pl.BlockSpec(shape, lambda k: (0,) * len(shape))
    return pl.pallas_call(
        tile_body,
        grid=(n,),
        out_shape=(
            jax.ShapeDtypeStruct((n * IB * nj, CP), BF),
            jax.ShapeDtypeStruct((CL * CL, CP), F32),
            jax.ShapeDtypeStruct((8, CP), F32),
            jax.ShapeDtypeStruct((seqs, CL * nj), BF),
            jax.ShapeDtypeStruct((seqs, n * IB * CL), BF),
        ),
        in_specs=[
            pl.BlockSpec((seqs, IB * CL), lambda k: (0, k)),
            whole(seqs, CL * nj),
            pl.BlockSpec((IB * nj, CP), lambda k: (k, 0)),
            whole(CL * CL, CP),
            whole(CP, CL * CL),
            whole(1, CP),
        ],
        out_specs=(
            pl.BlockSpec((IB * nj, CP), lambda k: (k, 0)),
            whole(CL * CL, CP),
            whole(8, CP),
            whole(seqs, CL * nj),
            pl.BlockSpec((seqs, IB * CL), lambda k: (0, k)),
        ),
        scratch_shapes=[
            pltpu.VMEM((CL * CL, IB * nj), BF),
            pltpu.VMEM((IB * CL, CL * nj), BF),
            pltpu.VMEM((seqs, CL * nj), F32),
        ],
        compiler_params=pltpu.CompilerParams(
            dimension_semantics=("arbitrary",), vmem_limit_bytes=40 << 20
        ),
        name="tile",
    )(left, right, dpair, w, wt, bias)


def shards(left, right, weight, bias, cotangent):
    nrow, ncol = lax.axis_size("row"), lax.axis_size("col")
    srow, scol = right.shape[0], left.shape[0]
    seqs = srow * nrow
    ni, nj = cotangent.shape[0], cotangent.shape[1]

    def gather(x, axis, n):
        y = jnp.broadcast_to(x[None], (n,) + x.shape)
        return lax.all_to_all(y, axis, 0, 0, tiled=True).reshape(seqs, x.shape[1])

    right_ej = right.reshape(srow, nj, CL).transpose(0, 2, 1).reshape(srow, CL * nj)
    left_full = gather(left, "col", ncol)
    right_full = gather(right_ej, "row", nrow)
    w = weight.reshape(CL, CL, CP).transpose(1, 0, 2).reshape(CL * CL, CP)
    pair, gw, gb, gr, gl = tile(
        left_full, right_full, cotangent.reshape(ni * nj, CP), w, w.T, bias.reshape(1, CP)
    )

    def scatter(x, axis, n):
        y = lax.all_to_all(x.reshape(n, seqs // n, x.shape[1]), axis, 0, 0, tiled=True)
        return jnp.sum(y.astype(F32), axis=0).astype(BF)

    ndev = nrow * ncol
    rows = CL * CL // ndev
    gb = jnp.sum(gb, axis=0)
    tail = jnp.broadcast_to(gb, (ndev, 1, CP))
    both = jnp.concatenate([gw.reshape(ndev, rows, CP), tail], axis=1)
    both = jnp.sum(lax.all_to_all(both, ("row", "col"), 0, 0, tiled=True), axis=0)
    grad_left = scatter(gl, "col", ncol)
    grad_right = scatter(gr, "row", nrow).reshape(srow, CL, nj).transpose(0, 2, 1)
    part = jnp.broadcast_to(both[None, :rows], (ndev, rows, CP))
    gw = lax.all_to_all(part, ("row", "col"), 0, 0, tiled=True)
    gw = gw.reshape(CL, CL, CP).transpose(1, 0, 2).reshape(CL * CL, CP)
    return (
        pair.reshape(ni, nj, CP),
        grad_left,
        grad_right.reshape(srow, nj * CL),
        gw,
        both[rows],
    )


def solution(mesh):
    placed = (P("col", "row"), P("row", "col"), P(), P(), P("row", "col", None))
    return jax.shard_map(
        shards,
        mesh=mesh,
        in_specs=placed,
        out_specs=(P("row", "col", None), P("col", "row"), P("row", "col"), P(), P()),
        check_vma=False,
    )
```

```python
import jax
import jax.numpy as jnp
from jax import lax
from jax.experimental import pallas as pl
from jax.experimental.pallas import tpu as pltpu
from jax.sharding import PartitionSpec as P


CL = 32
CP = 128
FB = 16
IB = 8
EB = 8
BF = jnp.bfloat16
F32 = jnp.float32

NX, NZ, NC, NY = 4, 2, 2, 4


def row_shift(dx, dz, dc):
    place = lambda x, z, c: (x * NZ + z) * NC + c
    return [
        (place(x, z, c), place((x + dx) % NX, (z + dz) % NZ, (c + dc) % NC))
        for x in range(NX)
        for z in range(NZ)
        for c in range(NC)
    ]


def col_shift(dz, dy):
    return [(z * NY + y, (z + dz) % NZ * NY + (y + dy) % NY) for z in range(NZ) for y in range(NY)]


def dot(a, b, ca, cb):
    return lax.dot_general(a, b, (((ca,), (cb,)), ((), ())), preferred_element_type=F32)


def whole(*shape):
    return pl.BlockSpec(shape, lambda k: (0,) * len(shape))


def left_block(pieces, l_s):
    col = lax.axis_index("col")
    z, y = col // NY, col % NY
    for d in range(NY):
        for b in range(NZ):
            l_s[(z + b) % NZ * NY + (y + NY - d) % NY] = pieces[d][b]
    return l_s[...].reshape(l_s.shape[0] * l_s.shape[1], l_s.shape[2])


def forward_body(l0, l1, l2, l3, r_ref, d_ref, wt_ref, b_ref, p_ref, gw_ref, gb_ref, rt_ref, l_s):
    k = pl.program_id(0)
    nj = d_ref.shape[0] // FB
    left = left_block((l0, l1, l2, l3), l_s).T
    scale = 1.0 / left.shape[1]
    part = rt_ref.shape[0]
    rt_ref[...] = r_ref[:, pl.ds(pl.multiple_of(k * part, part), part)].T
    rows = []
    for eb in range(CL // EB):
        t = dot(left, r_ref[:, eb * EB * nj : (eb + 1) * EB * nj], 1, 0)
        t = (t * scale).astype(BF)
        for e1 in range(EB):
            rows.append(
                jnp.concatenate(
                    [t[i * CL : (i + 1) * CL, e1 * nj : (e1 + 1) * nj] for i in range(FB)], axis=1
                )
            )
    outer = jnp.concatenate(rows, axis=0)
    p_ref[...] = (dot(wt_ref[...], outer, 1, 0).T + b_ref[...]).astype(BF)
    gw = dot(outer, d_ref[...], 1, 0)
    gb = jnp.sum(d_ref[...].astype(F32).reshape(-1, 8, CP), axis=0)

    @pl.when(k == 0)
    def _():
        gw_ref[...] = gw
        gb_ref[...] = gb

    @pl.when(k != 0)
    def _():
        gw_ref[...] += gw
        gb_ref[...] += gb


def backward_body(
    l0, l1, l2, l3, rt_ref, d_ref, w_ref, g0, g1, g2, g3, keep_ref, send_ref, l_s, gl_s, acc
):
    k = pl.program_id(0)
    nj = d_ref.shape[0] // IB
    left = left_block((l0, l1, l2, l3), l_s)
    scale = 1.0 / left.shape[0]
    rows = []
    for q in range(IB // 2):
        t = dot(w_ref[...], d_ref[q * 2 * nj : (q + 1) * 2 * nj, :], 1, 1).astype(BF)
        for i2 in range(2):
            rows.append(
                jnp.concatenate(
                    [t[e * CL : (e + 1) * CL, i2 * nj : (i2 + 1) * nj] for e in range(CL)], axis=1
                )
            )
    grad = jnp.concatenate(rows, axis=0)
    gl_s[...] = (dot(grad, rt_ref[...], 1, 0) * scale).T.reshape(gl_s.shape)
    col = lax.axis_index("col")
    z, y = col // NY, col % NY
    for d, out in enumerate((g0, g1, g2, g3)):
        for b in range(NZ):
            out[b] = gl_s[(z + b) % NZ * NY + (y + d) % NY].astype(out.dtype)
    gr = dot(left, grad, 1, 0).reshape(acc.shape)

    @pl.when(k == 0)
    def _():
        acc[...] = gr

    @pl.when(k != 0)
    def _():
        acc[...] += gr

    @pl.when(k == pl.num_programs(0) - 1)
    def _():
        row = lax.axis_index("row")
        x, zh, core = row // (NZ * NC), row // NC % NZ, row % NC
        for dx in range(NX):
            for b in range(NZ):
                at = ((x + dx) % NX * NZ + (zh + b) % NZ) * NC
                keep_ref[dx * NZ + b] = acc[at + core] * scale
                send_ref[dx * NZ + b] = (acc[at + 1 - core] * scale).astype(BF)


def params(mib):
    return pltpu.CompilerParams(dimension_semantics=("arbitrary",), vmem_limit_bytes=mib << 20)


def forward(pieces, right, dpair, wt, bias):
    scol, width = pieces[0].shape[1:]
    seqs, nj = right.shape[0], right.shape[1] // CL
    n = width // (FB * CL)
    return pl.pallas_call(
        forward_body,
        grid=(n,),
        out_shape=(
            jax.ShapeDtypeStruct((n * FB * nj, CP), BF),
            pltpu.HBM((CL * CL, CP), F32),
            jax.ShapeDtypeStruct((8, CP), F32),
            pltpu.HBM((CL * nj, seqs), BF),
        ),
        in_specs=[pl.BlockSpec((NZ, scol, FB * CL), lambda k: (0, 0, k))] * NY
        + [
            whole(seqs, CL * nj),
            pl.BlockSpec((FB * nj, CP), lambda k: (k, 0)),
            whole(CP, CL * CL),
            whole(1, CP),
        ],
        out_specs=(
            pl.BlockSpec((FB * nj, CP), lambda k: (k, 0)),
            whole(CL * CL, CP),
            whole(8, CP),
            pl.BlockSpec((CL * nj // n, seqs), lambda k: (k, 0)),
        ),
        scratch_shapes=[pltpu.VMEM((NZ * NY, scol, FB * CL), BF)],
        compiler_params=params(40),
        name="forward",
    )(*pieces, right, dpair, wt, bias)


def backward(pieces, right_t, dpair, w):
    scol, width = pieces[0].shape[1:]
    seqs, nj = right_t.shape[1], right_t.shape[0] // CL
    n = width // (IB * CL)
    srow = seqs // (NX * NZ * NC)
    gl_spec = pl.BlockSpec((NZ, scol, IB * CL), lambda k: (0, 0, k))
    half = (NX * NZ, srow, CL * nj)
    return pl.pallas_call(
        backward_body,
        grid=(n,),
        out_shape=(
            pltpu.HBM((NZ, scol, width), F32),
            pltpu.HBM((NZ, scol, width), BF),
            pltpu.HBM((NZ, scol, width), BF),
            pltpu.HBM((NZ, scol, width), BF),
            pltpu.HBM(half, F32),
            pltpu.HBM(half, BF),
        ),
        in_specs=[pl.BlockSpec((NZ, scol, IB * CL), lambda k: (0, 0, k))] * NY
        + [
            whole(CL * nj, seqs),
            pl.BlockSpec((IB * nj, CP), lambda k: (k, 0)),
            whole(CL * CL, CP),
        ],
        out_specs=(gl_spec,) * NY + (whole(*half),) * 2,
        scratch_shapes=[
            pltpu.VMEM((NZ * NY, scol, IB * CL), BF),
            pltpu.VMEM((NZ * NY, scol, IB * CL), F32),
            pltpu.VMEM((NX * NZ * NC, srow, CL * nj), F32),
        ],
        compiler_params=params(24),
        name="backward",
    )(*pieces, right_t, dpair, w)


def shards(left, right, weight, bias, cotangent):
    ndev = lax.axis_size("row") * lax.axis_size("col")
    srow = right.shape[0]
    seqs = srow * lax.axis_size("row")
    ni, nj = cotangent.shape[0], cotangent.shape[1]
    same_core = [[xz * NC + c for xz in range(NX * NZ)] for c in range(NC)]
    core = lax.axis_index("row") & 1

    other = lax.ppermute(left, "col", col_shift(1, 0))
    mine = right.reshape(srow, nj, CL).transpose(0, 2, 1).reshape(1, srow, CL * nj)
    mine = jnp.broadcast_to(mine, (NX * NZ, srow, CL * nj))
    mine = lax.all_to_all(mine, "row", 0, 0, tiled=True, axis_index_groups=same_core)
    pair = jnp.stack([left, other])
    pieces = [pair] + [lax.ppermute(pair, "col", col_shift(0, d)) for d in range(1, NY)]
    theirs = lax.ppermute(mine, "row", row_shift(0, 0, 1))
    first = jnp.where(core == 0, mine, theirs)
    second = jnp.where(core == 0, theirs, mine)
    right_full = jnp.stack([first, second], axis=1).reshape(seqs, CL * nj)

    dpair = cotangent.reshape(ni * nj, CP)
    w = weight.reshape(CL, CL, CP).transpose(1, 0, 2).reshape(CL * CL, CP)
    pair_update, gw, gb, right_t = forward(pieces, right_full, dpair, w.T, bias.reshape(1, CP))

    rows = CL * CL // ndev
    gw, dpair = lax.optimization_barrier((gw, dpair))
    gw = lax.all_to_all(gw.reshape(ndev, rows, CP), ("row", "col"), 0, 0, tiled=True)
    gw = jnp.concatenate([jnp.sum(gw, axis=0), jnp.sum(gb, axis=0, keepdims=True)], axis=0)

    l0, l1, l2, l3, keep, send = backward(pieces, right_t, dpair, w)

    gw = jnp.broadcast_to(gw.reshape(1, 1, (rows + 1) * CP), (ndev, 1, (rows + 1) * CP))
    gw = lax.all_to_all(gw, ("row", "col"), 0, 0, tiled=True)
    grad_b = jnp.sum(gw[:, 0, rows * CP :], axis=0)
    grad_w = gw[:, 0, : rows * CP].reshape(CL, CL, CP).transpose(1, 0, 2).reshape(CL * CL, CP)

    got = lax.ppermute(send, "row", row_shift(0, 0, 1))
    part = [keep[NZ * d : NZ * (d + 1)] + got[NZ * d : NZ * (d + 1)].astype(F32) for d in range(NX)]
    away = [p.astype(BF) for p in part[1:]]
    rgot = [lax.ppermute(p, "row", row_shift(d + 1, 0, 0)) for d, p in enumerate(away)]
    lgot = [lax.ppermute(g, "col", col_shift(0, d)) for d, g in ((1, l1), (2, l2), (3, l3))]
    lsum = l0 + sum(g.astype(F32) for g in lgot)
    lfar = lsum[1].astype(BF)
    lz = lax.ppermute(lfar, "col", col_shift(1, 0))
    rsum = part[0] + sum(g.astype(F32) for g in rgot)
    rfar = rsum[1].astype(BF)
    rz = lax.ppermute(rfar, "row", row_shift(0, 1, 0))
    grad_left = (lsum[0] + lz.astype(F32)).astype(BF)
    grad_right = (rsum[0] + rz.astype(F32)).astype(BF)
    grad_right = grad_right.reshape(srow, CL, nj).transpose(0, 2, 1).reshape(srow, nj * CL)
    return (pair_update.reshape(ni, nj, CP), grad_left, grad_right, grad_w, grad_b)


def solution(mesh):
    placed = (P("col", "row"), P("row", "col"), P(), P(), P("row", "col", None))
    return jax.shard_map(
        shards,
        mesh=mesh,
        in_specs=placed,
        out_specs=(P("row", "col", None), P("col", "row"), P("row", "col"), P(), P()),
        check_vma=False,
    )
```

```python
import jax
import jax.numpy as jnp
from jax import lax
from jax.experimental import pallas as pl
from jax.experimental.pallas import tpu as pltpu
from jax.sharding import PartitionSpec as P


CL = 32
CP = 128
FB = 16
IB = 8
EB = 8
GB = 1024
BF = jnp.bfloat16
F32 = jnp.float32

NX, NZ, NC, NY = 4, 2, 2, 4


def row_shift(dx, dz, dc):
    place = lambda x, z, c: (x * NZ + z) * NC + c
    return [
        (place(x, z, c), place((x + dx) % NX, (z + dz) % NZ, (c + dc) % NC))
        for x in range(NX)
        for z in range(NZ)
        for c in range(NC)
    ]


def col_shift(dz, dy):
    return [(z * NY + y, (z + dz) % NZ * NY + (y + dy) % NY) for z in range(NZ) for y in range(NY)]


def dot(a, b, ca, cb):
    return lax.dot_general(a, b, (((ca,), (cb,)), ((), ())), preferred_element_type=F32)


def whole(*shape):
    return pl.BlockSpec(shape, lambda k: (0,) * len(shape))


def left_block(pieces, l_s):
    col = lax.axis_index("col")
    z, y = col // NY, col % NY
    for d in range(NY):
        for b in range(NZ):
            l_s[(z + b) % NZ * NY + (y + NY - d) % NY] = pieces[d][b]
    return l_s[...].reshape(l_s.shape[0] * l_s.shape[1], l_s.shape[2])


def forward_body(*refs):
    l_refs, refs = refs[:NY], refs[NY:]
    own, other, refs = refs[:NX], refs[NX : 2 * NX], refs[2 * NX :]
    d_ref, wt_ref, b_ref, p_ref, out_ref, rt_ref, l_s, r_s, gw_s, gb_s = refs
    k = pl.program_id(0)
    nj = d_ref.shape[0] // FB

    @pl.when(k == 0)
    def _():
        gw_s[...] = jnp.zeros_like(gw_s)
        gb_s[...] = jnp.zeros_like(gb_s)
        row = lax.axis_index("row")
        x, zh, core = row // (NZ * NC), row // NC % NZ, row % NC
        for d in range(NX):
            for b in range(NZ):
                at = ((x + NX - d) % NX * NZ + (zh + b) % NZ) * NC
                r_s[at + core] = own[d][b]
                r_s[at + 1 - core] = other[d][b]

    left = left_block(l_refs, l_s).T
    seqs = left.shape[1]
    scale = 1.0 / seqs
    part = rt_ref.shape[0]
    turn = r_s[:, :, pl.ds(pl.multiple_of(k * part, part), part)]
    rt_ref[...] = turn.reshape(seqs, part).T
    rows = []
    for eb in range(CL // EB):
        right = r_s[:, :, eb * EB * nj : (eb + 1) * EB * nj].reshape(seqs, EB * nj)
        t = dot(left, right, 1, 0)
        t = (t * scale).astype(BF)
        for e1 in range(EB):
            rows.append(
                jnp.concatenate(
                    [t[i * CL : (i + 1) * CL, e1 * nj : (e1 + 1) * nj] for i in range(FB)], axis=1
                )
            )
    outer = jnp.concatenate(rows, axis=0)
    p_ref[...] = (dot(wt_ref[...], outer, 1, 0).T + b_ref[...]).astype(BF)
    gw = dot(outer, d_ref[...], 1, 0)
    gb = jnp.sum(d_ref[...].astype(F32).reshape(-1, 8, CP), axis=0)

    gw_s[...] += gw
    gb_s[...] += gb

    @pl.when(k == pl.num_programs(0) - 1)
    def _():
        total = jnp.sum(gb_s[...], axis=0, keepdims=True)
        high = total.astype(BF).astype(F32)
        middle = (total - high).astype(BF).astype(F32)
        at = lax.broadcasted_iota(jnp.int32, gb_s.shape, 0)
        tail = jnp.where(at == 0, high, jnp.where(at == 1, middle, total - high - middle))
        tail = jnp.where(at < 3, tail, 0.0).astype(BF)
        ndev, rows = out_ref.shape[0], out_ref.shape[1] - 8
        for dev in range(ndev):
            c, e = divmod(dev * rows, CL)
            out_ref[dev, :rows] = gw_s[pl.ds(e * CL + c, rows, stride=CL), :].astype(BF)
            out_ref[dev, rows:] = tail


def weight_body(x_ref, gw_ref, gb_ref):
    total = jnp.sum(x_ref[...].astype(F32), axis=0)
    gw_ref[...] = jnp.broadcast_to(total[None, :-8], gw_ref.shape)
    gb_ref[...] = jnp.sum(total[-8:], axis=0, keepdims=True)


def backward_body(
    l0, l1, l2, l3, rt_ref, d_ref, w_ref, g0, g1, g2, g3, keep_ref, send_ref, l_s, gl_s, acc
):
    k = pl.program_id(0)
    nj = d_ref.shape[0] // IB

    @pl.when(k == 0)
    def _():
        acc[...] = jnp.zeros_like(acc)

    left = left_block((l0, l1, l2, l3), l_s)
    scale = 1.0 / left.shape[0]
    rows = []
    for q in range(IB // 2):
        t = dot(w_ref[...], d_ref[q * 2 * nj : (q + 1) * 2 * nj, :], 1, 1).astype(BF)
        for i2 in range(2):
            rows.append(
                jnp.concatenate(
                    [t[e * CL : (e + 1) * CL, i2 * nj : (i2 + 1) * nj] for e in range(CL)], axis=1
                )
            )
    grad = jnp.concatenate(rows, axis=0)
    gl_s[...] = (dot(grad, rt_ref[...], 1, 0) * scale).T.reshape(gl_s.shape)
    col = lax.axis_index("col")
    z, y = col // NY, col % NY
    for d, out in enumerate((g0, g1, g2, g3)):
        for b in range(NZ):
            out[b] = gl_s[(z + b) % NZ * NY + (y + d) % NY].astype(out.dtype)
    for at in range(0, CL * nj, GB):
        gr = dot(left, grad[:, at : at + GB], 1, 0)
        acc[:, :, at : at + GB] += gr.reshape(acc.shape[:2] + (GB,))

    @pl.when(k == pl.num_programs(0) - 1)
    def _():
        row = lax.axis_index("row")
        x, zh, core = row // (NZ * NC), row // NC % NZ, row % NC
        for dx in range(NX):
            for b in range(NZ):
                at = ((x + dx) % NX * NZ + (zh + b) % NZ) * NC
                keep_ref[dx * NZ + b] = acc[at + core] * scale
                send_ref[dx * NZ + b] = (acc[at + 1 - core] * scale).astype(BF)


def params(mib):
    return pltpu.CompilerParams(dimension_semantics=("arbitrary",), vmem_limit_bytes=mib << 20)


def forward(pieces, own, other, dpair, wt, bias, ndev):
    scol, width = pieces[0].shape[1:]
    srow = own[0].shape[1]
    seqs, nj = scol * NZ * NY, own[0].shape[2] // CL
    n = width // (FB * CL)
    return pl.pallas_call(
        forward_body,
        grid=(n,),
        out_shape=(
            jax.ShapeDtypeStruct((n * FB * nj, CP), BF),
            pltpu.HBM((ndev, CL * CL // ndev + 8, CP), BF),
            pltpu.HBM((CL * nj, seqs), BF),
        ),
        in_specs=[pl.BlockSpec((NZ, scol, FB * CL), lambda k: (0, 0, k))] * NY
        + [whole(NZ, srow, CL * nj)] * (2 * NX)
        + [
            pl.BlockSpec((FB * nj, CP), lambda k: (k, 0)),
            whole(CP, CL * CL),
            whole(1, CP),
        ],
        out_specs=(
            pl.BlockSpec((FB * nj, CP), lambda k: (k, 0)),
            whole(ndev, CL * CL // ndev + 8, CP),
            pl.BlockSpec((CL * nj // n, seqs), lambda k: (k, 0)),
        ),
        scratch_shapes=[
            pltpu.VMEM((NZ * NY, scol, FB * CL), BF),
            pltpu.VMEM((NX * NZ * NC, srow, CL * nj), BF),
            pltpu.VMEM((CL * CL, CP), F32),
            pltpu.VMEM((8, CP), F32),
        ],
        compiler_params=params(40),
        name="forward",
    )(*pieces, *own, *other, dpair, wt, bias)


def backward(pieces, right_t, dpair, w):
    scol, width = pieces[0].shape[1:]
    seqs, nj = right_t.shape[1], right_t.shape[0] // CL
    n = width // (IB * CL)
    srow = seqs // (NX * NZ * NC)
    gl_spec = pl.BlockSpec((NZ, scol, IB * CL), lambda k: (0, 0, k))
    half = (NX * NZ, srow, CL * nj)
    return pl.pallas_call(
        backward_body,
        grid=(n,),
        out_shape=(
            pltpu.HBM((NZ, scol, width), F32),
            pltpu.HBM((NZ, scol, width), BF),
            pltpu.HBM((NZ, scol, width), BF),
            pltpu.HBM((NZ, scol, width), BF),
            pltpu.HBM(half, F32),
            pltpu.HBM(half, BF),
        ),
        in_specs=[pl.BlockSpec((NZ, scol, IB * CL), lambda k: (0, 0, k))] * NY
        + [
            whole(CL * nj, seqs),
            pl.BlockSpec((IB * nj, CP), lambda k: (k, 0)),
            whole(CL * CL, CP),
        ],
        out_specs=(gl_spec,) * NY + (whole(*half),) * 2,
        scratch_shapes=[
            pltpu.VMEM((NZ * NY, scol, IB * CL), BF),
            pltpu.VMEM((NZ * NY, scol, IB * CL), F32),
            pltpu.VMEM((NX * NZ * NC, srow, CL * nj), F32),
        ],
        compiler_params=params(24),
        name="backward",
    )(*pieces, right_t, dpair, w)


def shards(left, right, weight, bias, cotangent):
    ndev = lax.axis_size("row") * lax.axis_size("col")
    srow = right.shape[0]
    ni, nj = cotangent.shape[0], cotangent.shape[1]

    other = lax.ppermute(left, "col", col_shift(1, 0))
    mine = right.reshape(srow, nj, CL).transpose(0, 2, 1).reshape(srow, CL * nj)
    theirs = lax.ppermute(mine, "row", row_shift(0, 1, 0))
    pair = jnp.stack([left, other])
    pieces = [pair] + [lax.ppermute(pair, "col", col_shift(0, d)) for d in range(1, NY)]
    pair = jnp.stack([mine, theirs])
    mine = [pair] + [lax.ppermute(pair, "row", row_shift(d, 0, 0)) for d in range(1, NX)]
    theirs = [lax.ppermute(p, "row", row_shift(0, 0, 1)) for p in mine]

    dpair = cotangent.reshape(ni * nj, CP)
    w = weight.reshape(CL, CL, CP).transpose(1, 0, 2).reshape(CL * CL, CP)
    wt = w.T
    pair_update, share, right_t = forward(
        pieces, mine, theirs, dpair, wt, bias.reshape(1, CP), ndev
    )
    share, dpair = lax.optimization_barrier((share, dpair))
    share = lax.all_to_all(share, ("row", "col"), 0, 0, tiled=True)
    l0, l1, l2, l3, keep, send = backward(pieces, right_t, dpair, w)
    own, grad_b = pl.pallas_call(
        weight_body,
        out_shape=(pltpu.HBM((ndev, CL * CL // ndev, CP), F32), jax.ShapeDtypeStruct((1, CP), F32)),
        name="weight",
    )(share)
    grad_w = lax.all_to_all(own, ("row", "col"), 0, 0, tiled=True).reshape(CL * CL, CP)
    grad_b = grad_b.reshape(CP)

    got = lax.ppermute(send, "row", row_shift(0, 0, 1))
    part = [keep[NZ * d : NZ * (d + 1)] + got[NZ * d : NZ * (d + 1)].astype(F32) for d in range(NX)]
    away = [p.astype(BF) for p in part[1:]]
    rgot = [lax.ppermute(p, "row", row_shift(d + 1, 0, 0)) for d, p in enumerate(away)]
    lgot = [lax.ppermute(g, "col", col_shift(0, d)) for d, g in ((1, l1), (2, l2), (3, l3))]
    lsum = l0 + sum(g.astype(F32) for g in lgot)
    lfar = lsum[1].astype(BF)
    lz = lax.ppermute(lfar, "col", col_shift(1, 0))
    rsum = part[0] + sum(g.astype(F32) for g in rgot)
    rfar = rsum[1].astype(BF)
    rz = lax.ppermute(rfar, "row", row_shift(0, 1, 0))
    grad_left = (lsum[0] + lz.astype(F32)).astype(BF)
    grad_right = (rsum[0] + rz.astype(F32)).astype(BF)
    grad_right = grad_right.reshape(srow, CL, nj).transpose(0, 2, 1).reshape(srow, nj * CL)
    return (pair_update.reshape(ni, nj, CP), grad_left, grad_right, grad_w, grad_b)


def solution(mesh):
    placed = (P("col", "row"), P("row", "col"), P(), P(), P("row", "col", None))
    return jax.shard_map(
        shards,
        mesh=mesh,
        in_specs=placed,
        out_specs=(P("row", "col", None), P("col", "row"), P("row", "col"), P(), P()),
        check_vma=False,
    )
```

```python
import jax
import jax.numpy as jnp
from jax import lax
from jax.experimental import pallas as pl
from jax.experimental.pallas import tpu as pltpu
from jax.sharding import PartitionSpec as P


CL = 32
CP = 128
FB = 16
IB = 8
EB = 8
GB = 1024
BF = jnp.bfloat16
F32 = jnp.float32

NX, NZ, NC, NY = 4, 2, 2, 4


def row_shift(dx, dz, dc):
    place = lambda x, z, c: (x * NZ + z) * NC + c
    return [
        (place(x, z, c), place((x + dx) % NX, (z + dz) % NZ, (c + dc) % NC))
        for x in range(NX)
        for z in range(NZ)
        for c in range(NC)
    ]


def col_shift(dz, dy):
    return [(z * NY + y, (z + dz) % NZ * NY + (y + dy) % NY) for z in range(NZ) for y in range(NY)]


def dot(a, b, ca, cb):
    return lax.dot_general(a, b, (((ca,), (cb,)), ((), ())), preferred_element_type=F32)


def whole(*shape):
    return pl.BlockSpec(shape, lambda k: (0,) * len(shape))


def left_block(pieces, l_s):
    col = lax.axis_index("col")
    z, y = col // NY, col % NY
    for d in range(NY):
        for b in range(NZ):
            l_s[(z + b) % NZ * NY + (y + NY - d) % NY] = pieces[d][b]
    return l_s[...].reshape(l_s.shape[0] * l_s.shape[1], l_s.shape[2])


def forward_body(*refs):
    l_refs, refs = refs[:NY], refs[NY:]
    own, other, refs = refs[:NX], refs[NX : 2 * NX], refs[2 * NX :]
    d_ref, wt_ref, b_ref, p_ref, out_ref, rt_ref, l_s, r_s, gw_s, gb_s = refs
    k = pl.program_id(0)
    nj = d_ref.shape[0] // FB

    @pl.when(k == 0)
    def _():
        gw_s[...] = jnp.zeros_like(gw_s)
        gb_s[...] = jnp.zeros_like(gb_s)
        row = lax.axis_index("row")
        x, zh, core = row // (NZ * NC), row // NC % NZ, row % NC
        for d in range(NX):
            for b in range(NZ):
                at = ((x + NX - d) % NX * NZ + (zh + b) % NZ) * NC
                r_s[at + core] = own[d][b]
                r_s[at + 1 - core] = other[d][b]

    left = left_block(l_refs, l_s).T
    seqs = left.shape[1]
    scale = 1.0 / seqs
    part = rt_ref.shape[0]
    turn = r_s[:, :, pl.ds(pl.multiple_of(k * part, part), part)]
    rt_ref[...] = turn.reshape(seqs, part).T
    rows = []
    for eb in range(CL // EB):
        right = r_s[:, :, eb * EB * nj : (eb + 1) * EB * nj].reshape(seqs, EB * nj)
        t = dot(left, right, 1, 0)
        t = (t * scale).astype(BF)
        for e1 in range(EB):
            rows.append(
                jnp.concatenate(
                    [t[i * CL : (i + 1) * CL, e1 * nj : (e1 + 1) * nj] for i in range(FB)], axis=1
                )
            )
    outer = jnp.concatenate(rows, axis=0)
    p_ref[...] = (dot(wt_ref[...], outer, 1, 0).T + b_ref[...]).astype(BF)
    gw = dot(outer, d_ref[...], 1, 0)
    gb = jnp.sum(d_ref[...].astype(F32).reshape(-1, 8, CP), axis=0)

    gw_s[...] += gw
    gb_s[...] += gb

    @pl.when(k == pl.num_programs(0) - 1)
    def _():
        total = jnp.sum(gb_s[...], axis=0, keepdims=True)
        high = total.astype(BF).astype(F32)
        middle = (total - high).astype(BF).astype(F32)
        at = lax.broadcasted_iota(jnp.int32, gb_s.shape, 0)
        tail = jnp.where(at == 0, high, jnp.where(at == 1, middle, total - high - middle))
        tail = jnp.where(at < 3, tail, 0.0).astype(BF)
        ndev, rows = out_ref.shape[0], out_ref.shape[1] - 8
        for dev in range(ndev):
            c, e = divmod(dev * rows, CL)
            out_ref[dev, :rows] = gw_s[pl.ds(e * CL + c, rows, stride=CL), :].astype(BF)
            out_ref[dev, rows:] = tail


def weight_body(x_ref, gw_ref, gb_ref):
    total = jnp.sum(x_ref[...].astype(F32), axis=0)
    gw_ref[...] = jnp.broadcast_to(total[None, :-8].astype(BF), gw_ref.shape)
    gb_ref[...] = jnp.sum(total[-8:], axis=0, keepdims=True)


def backward_body(
    l0, l1, l2, l3, rt_ref, d_ref, w_ref, g0, g1, g2, g3, keep_ref, send_ref, l_s, gl_s, acc
):
    k = pl.program_id(0)
    nj = d_ref.shape[0] // IB

    @pl.when(k == 0)
    def _():
        acc[...] = jnp.zeros_like(acc)

    left = left_block((l0, l1, l2, l3), l_s)
    scale = 1.0 / left.shape[0]
    rows = []
    for q in range(IB // 2):
        t = dot(w_ref[...], d_ref[q * 2 * nj : (q + 1) * 2 * nj, :], 1, 1).astype(BF)
        for i2 in range(2):
            rows.append(
                jnp.concatenate(
                    [t[e * CL : (e + 1) * CL, i2 * nj : (i2 + 1) * nj] for e in range(CL)], axis=1
                )
            )
    grad = jnp.concatenate(rows, axis=0)
    gl_s[...] = (dot(grad, rt_ref[...], 1, 0) * scale).T.reshape(gl_s.shape)
    col = lax.axis_index("col")
    z, y = col // NY, col % NY
    for d, out in enumerate((g0, g1, g2, g3)):
        for b in range(NZ):
            out[b] = gl_s[(z + b) % NZ * NY + (y + d) % NY].astype(out.dtype)
    for at in range(0, CL * nj, GB):
        gr = dot(left, grad[:, at : at + GB], 1, 0)
        acc[:, :, at : at + GB] += gr.reshape(acc.shape[:2] + (GB,))

    @pl.when(k == pl.num_programs(0) - 1)
    def _():
        row = lax.axis_index("row")
        x, zh, core = row // (NZ * NC), row // NC % NZ, row % NC
        for dx in range(NX):
            for b in range(NZ):
                at = ((x + dx) % NX * NZ + (zh + b) % NZ) * NC
                keep_ref[dx * NZ + b] = acc[at + core] * scale
                send_ref[dx * NZ + b] = (acc[at + 1 - core] * scale).astype(BF)


def params(mib):
    return pltpu.CompilerParams(dimension_semantics=("arbitrary",), vmem_limit_bytes=mib << 20)


def forward(pieces, own, other, dpair, wt, bias, ndev):
    scol, width = pieces[0].shape[1:]
    srow = own[0].shape[1]
    seqs, nj = scol * NZ * NY, own[0].shape[2] // CL
    n = width // (FB * CL)
    return pl.pallas_call(
        forward_body,
        grid=(n,),
        out_shape=(
            jax.ShapeDtypeStruct((n * FB * nj, CP), BF),
            pltpu.HBM((ndev, CL * CL // ndev + 8, CP), BF),
            pltpu.HBM((CL * nj, seqs), BF),
        ),
        in_specs=[pl.BlockSpec((NZ, scol, FB * CL), lambda k: (0, 0, k))] * NY
        + [whole(NZ, srow, CL * nj)] * (2 * NX)
        + [
            pl.BlockSpec((FB * nj, CP), lambda k: (k, 0)),
            whole(CP, CL * CL),
            whole(1, CP),
        ],
        out_specs=(
            pl.BlockSpec((FB * nj, CP), lambda k: (k, 0)),
            whole(ndev, CL * CL // ndev + 8, CP),
            pl.BlockSpec((CL * nj // n, seqs), lambda k: (k, 0)),
        ),
        scratch_shapes=[
            pltpu.VMEM((NZ * NY, scol, FB * CL), BF),
            pltpu.VMEM((NX * NZ * NC, srow, CL * nj), BF),
            pltpu.VMEM((CL * CL, CP), F32),
            pltpu.VMEM((8, CP), F32),
        ],
        compiler_params=params(40),
        name="forward",
    )(*pieces, *own, *other, dpair, wt, bias)


def backward(pieces, right_t, dpair, w):
    scol, width = pieces[0].shape[1:]
    seqs, nj = right_t.shape[1], right_t.shape[0] // CL
    n = width // (IB * CL)
    srow = seqs // (NX * NZ * NC)
    gl_spec = pl.BlockSpec((NZ, scol, IB * CL), lambda k: (0, 0, k))
    half = (NX * NZ, srow, CL * nj)
    return pl.pallas_call(
        backward_body,
        grid=(n,),
        out_shape=(
            pltpu.HBM((NZ, scol, width), F32),
            pltpu.HBM((NZ, scol, width), BF),
            pltpu.HBM((NZ, scol, width), BF),
            pltpu.HBM((NZ, scol, width), BF),
            pltpu.HBM(half, F32),
            pltpu.HBM(half, BF),
        ),
        in_specs=[pl.BlockSpec((NZ, scol, IB * CL), lambda k: (0, 0, k))] * NY
        + [
            whole(CL * nj, seqs),
            pl.BlockSpec((IB * nj, CP), lambda k: (k, 0)),
            whole(CL * CL, CP),
        ],
        out_specs=(gl_spec,) * NY + (whole(*half),) * 2,
        scratch_shapes=[
            pltpu.VMEM((NZ * NY, scol, IB * CL), BF),
            pltpu.VMEM((NZ * NY, scol, IB * CL), F32),
            pltpu.VMEM((NX * NZ * NC, srow, CL * nj), F32),
        ],
        compiler_params=params(24),
        name="backward",
    )(*pieces, right_t, dpair, w)


def shards(left, right, weight, bias, cotangent):
    ndev = lax.axis_size("row") * lax.axis_size("col")
    srow = right.shape[0]
    ni, nj = cotangent.shape[0], cotangent.shape[1]

    other = lax.ppermute(left, "col", col_shift(1, 0))
    mine = right.reshape(srow, nj, CL).transpose(0, 2, 1).reshape(srow, CL * nj)
    theirs = lax.ppermute(mine, "row", row_shift(0, 1, 0))
    pair = jnp.stack([left, other])
    pieces = [pair] + [lax.ppermute(pair, "col", col_shift(0, d)) for d in range(1, NY)]
    pair = jnp.stack([mine, theirs])
    mine = [pair] + [lax.ppermute(pair, "row", row_shift(d, 0, 0)) for d in range(1, NX)]
    theirs = [lax.ppermute(p, "row", row_shift(0, 0, 1)) for p in mine]

    dpair = cotangent.reshape(ni * nj, CP)
    w = weight.reshape(CL, CL, CP).transpose(1, 0, 2).reshape(CL * CL, CP)
    wt = w.T
    pair_update, share, right_t = forward(
        pieces, mine, theirs, dpair, wt, bias.reshape(1, CP), ndev
    )
    share, dpair = lax.optimization_barrier((share, dpair))
    share = lax.all_to_all(share, ("row", "col"), 0, 0, tiled=True)
    l0, l1, l2, l3, keep, send = backward(pieces, right_t, dpair, w)
    own, grad_b = pl.pallas_call(
        weight_body,
        out_shape=(pltpu.HBM((ndev, CL * CL // ndev, CP), BF), jax.ShapeDtypeStruct((1, CP), F32)),
        name="weight",
    )(share)
    grad_w = lax.all_to_all(own, ("row", "col"), 0, 0, tiled=True)
    grad_w = grad_w.reshape(CL * CL, CP).astype(F32)
    grad_b = grad_b.reshape(CP)

    got = lax.ppermute(send, "row", row_shift(0, 0, 1))
    part = [keep[NZ * d : NZ * (d + 1)] + got[NZ * d : NZ * (d + 1)].astype(F32) for d in range(NX)]
    away = [p.astype(BF) for p in part[1:]]
    rgot = [lax.ppermute(p, "row", row_shift(d + 1, 0, 0)) for d, p in enumerate(away)]
    lgot = [lax.ppermute(g, "col", col_shift(0, d)) for d, g in ((1, l1), (2, l2), (3, l3))]
    lsum = l0 + sum(g.astype(F32) for g in lgot)
    lfar = lsum[1].astype(BF)
    lz = lax.ppermute(lfar, "col", col_shift(1, 0))
    rsum = part[0] + sum(g.astype(F32) for g in rgot)
    rfar = rsum[1].astype(BF)
    rz = lax.ppermute(rfar, "row", row_shift(0, 1, 0))
    grad_left = (lsum[0] + lz.astype(F32)).astype(BF)
    grad_right = (rsum[0] + rz.astype(F32)).astype(BF)
    grad_right = grad_right.reshape(srow, CL, nj).transpose(0, 2, 1).reshape(srow, nj * CL)
    return (pair_update.reshape(ni, nj, CP), grad_left, grad_right, grad_w, grad_b)


def solution(mesh):
    placed = (P("col", "row"), P("row", "col"), P(), P(), P("row", "col", None))
    return jax.shard_map(
        shards,
        mesh=mesh,
        in_specs=placed,
        out_specs=(P("row", "col", None), P("col", "row"), P("row", "col"), P(), P()),
        check_vma=False,
    )
```
